32 devices in a mesh: node: 4 (over y, core), cores: 8 (over z, x).
Axes of the slice: x: 2, y: 2, z: 4, core: 2. Of those that a mesh axis runs over, the one named last changes fastest.
Arguments:
- adjoint: bfloat16 [256, 2, 128, 128], P(('node', 'cores')), may hold values from -6 to 6
- saved: bfloat16 [2, 4, 256, 2, 128, 128], P(None, None, ('node', 'cores')), may hold values from -0.046875 to 0.046875
- propagators: bfloat16 [2, 4, 2, 128, 128], replicated, may hold values from -3 to 3, as said below
- coupling: bfloat16 [128, 128], replicated, may hold values from -0.5 to 0.5
- higher: int32 [256, 4], replicated, may hold values from 0 to 255, as said below
- lower: int32 [256, 4], replicated, may hold values from 0 to 255, as said below
- ladder: int32 [2, 256, 4], P(None, ('node', 'cores')), may hold values from 0 to 3
- rates: float32 [2, 4], replicated, may hold values from 0.1 to 0.4
- decay: float32 [256], P(('node', 'cores')), may hold values from 0.4 to 1
Outputs:
- adjoint_out: bfloat16 [256, 2, 128, 128], P(('node', 'cores'))
- gradient: float32 [128, 8, 2, 128], P(('node', 'cores'))
The draws below stay inside these ranges and needn't reach their ends.
Inputs may be any that keep to these rules, and one draw needn't show every extreme that they name: Density j lives on owner j // 8. Taken in the order of density then mode, the 32 higher-tier partners of one owner's densities lie on distinct owners when 8 * 4 <= 32, and else exactly 1 of them lie on each owner. The same holds for the lower-tier partners. `propagators`: A propagator substep is close to unitary.
All inputs are finite; a program needn't handle non-finite values.
Results may differ from the reference program's by a relative error of at most 0.024.
Values may be sent and summed in bfloat16 or wider, within the bound.
A program may use at most 128 MiB of HBM per device.

```python
import math
import jax
import jax.numpy as jnp

DIM = 128
MODES = 4
ADO_DEV = 8
STEPS = 2
NSUB = 4
OWNERS = 32
NA = 256


def build_partners(key):
    links = ADO_DEV * MODES
    perm_key = jax.random.fold_in(key, 11)
    local_key = jax.random.fold_in(key, 12)
    perms = jax.vmap(lambda owner_id: jax.random.permutation(jax.random.fold_in(perm_key, owner_id), OWNERS))(jnp.arange(OWNERS))
    source = perms[:, jnp.arange(links) % OWNERS]
    local = jax.random.randint(local_key, (OWNERS, links), 0, ADO_DEV)
    return (source * ADO_DEV + local).reshape(OWNERS * ADO_DEV, MODES).astype(jnp.int32)


def draw_higher(key, part):
    return build_partners(jax.random.fold_in(key, 1))


def draw_lower(key, part):
    return build_partners(jax.random.fold_in(key, 2))


def draw_propagators(key, part):
    scale = 0.4 / DIM ** 0.5
    raw = jax.random.normal(key, (STEPS, NSUB, DIM, DIM), jnp.float32) * scale
    hermit = (raw + jnp.swapaxes(raw, -1, -2)) / 2.0 ** 0.5
    square = jnp.matmul(hermit, hermit)
    cube = jnp.matmul(square, hermit)
    identity = jnp.eye(DIM, dtype=jnp.float32)
    real_part = identity - 0.5 * square
    imag_part = -hermit + cube / 6.0
    return jnp.stack([real_part, imag_part], axis=2).astype(jnp.bfloat16)


def set_ends(values, own_key, least, high):
    extent = values.shape
    index_at = [jax.random.randint(jax.random.fold_in(own_key, axis), (), 0, extent[axis]) for axis in range(len(extent))]
    values = values.at[tuple(index_at)].set(least)
    longest = extent.index(max(extent))
    index_at[longest] = (index_at[longest] + 1) % extent[longest]
    return values.at[tuple(index_at)].set(high)


def with_spikes(array, rng, source, target, parts, factor):
    def block_of(position):
        return (jnp.arange(array.shape[position]) // (array.shape[position] // parts)).reshape((-1,) + (1,) * (array.ndim - 1 - position))

    first = jax.random.permutation(rng, parts)[block_of(target)]
    other_side = (block_of(target) + parts // 2) % parts
    return jnp.where((block_of(source) == first) | (block_of(source) == other_side), factor * array, array)


def level_of(key, extent, pieces, smallest, high):
    gain = 1.0
    for position, blocks in pieces:
        draws = jax.random.uniform(jax.random.fold_in(jax.random.fold_in(key, 6), position), (blocks,), jnp.float32, smallest / len(pieces), high / len(pieces))
        gain = gain * jnp.repeat(jnp.exp(draws), extent[position] // blocks).reshape((-1,) + (1,) * (len(extent) - 1 - position))
    return gain


def centred(rng, shape, deviation, bound, pieces=(), kind=jnp.bfloat16):
    gain = level_of(rng, shape, pieces, -0.22, 0.18) if pieces else 1.0
    drawn = jax.random.normal(rng, shape, jnp.float32) * deviation * gain
    return jnp.minimum(jnp.maximum(drawn, -bound), bound).astype(kind)


def gaussian_with(own_key, shape, width, limit, pieces, heavy, kind=jnp.bfloat16):
    entries = width * jax.random.normal(own_key, shape, jnp.float32)
    if pieces:
        entries = entries * level_of(own_key, shape, pieces, -0.22, 0.18)
    return jnp.clip(with_spikes(entries, jax.random.fold_in(own_key, 3), *heavy), -limit, limit).astype(kind)


def setup_inputs(seed: int = 0) -> dict:
    key_list = jax.random.split(jax.random.key(seed), 10)
    return {
        "adjoint": centred(key_list[0], (NA, 2, DIM, DIM), 1.0, 6.0, ((0, 32),)),
        "saved": gaussian_with(key_list[1], (STEPS, NSUB, NA, 2, DIM, DIM), (1.0 / (2 * DIM * NA) ** 0.5), 0.046875, ((2, 32),), (2, 5, 32, 2.75)),
        "propagators": draw_propagators(jax.random.fold_in(key_list[9], 71), 0),
        "coupling": centred(key_list[3], (DIM, DIM), DIM ** -0.5, 0.5),
        "higher": draw_higher(jax.random.fold_in(key_list[9], 71), 0),
        "lower": draw_lower(jax.random.fold_in(key_list[9], 71), 0),
        "ladder": set_ends(jax.random.randint(key_list[6], (2, NA, MODES), 0, 4), jax.random.fold_in(key_list[6], 1), 0, 3).astype(jnp.int32),
        "rates": jnp.clip(jnp.exp(jax.random.uniform(key_list[7], (2, MODES), jnp.float32, math.log(0.1), math.log(0.4))), 0.1, 0.4),
        "decay": jnp.clip(0.4 + 0.6 * jax.random.uniform(key_list[8], (NA,), jnp.float32) ** level_of(key_list[8], (NA,), ((0, 32),), -0.2, 0.2), 0.4, 1.0),
    }


def linked_sum(state_full, link_table, weights, strengths):
    total = jnp.zeros(state_full.shape, jnp.float32)
    for mode_index in range(MODES):
        factor = weights[:, mode_index].astype(jnp.float32) * strengths[mode_index]
        total = total + factor[:, None, None, None] * state_full[link_table[:, mode_index]]
    return total


def couple_step(state, up_sum, down_sum, coupling, decay):
    plus = (up_sum + down_sum).astype(jnp.bfloat16).astype(jnp.float32)
    minus = (up_sum - down_sum).astype(jnp.bfloat16).astype(jnp.float32)
    operator = coupling.astype(jnp.float32)
    left = jnp.einsum('ab,jxbc->jxac', operator, plus)
    right = jnp.einsum('jxab,bc->jxac', minus, operator)
    kept = decay[:, None, None, None] * state.astype(jnp.float32)
    real_part = kept[:, 0] + left[:, 1] - right[:, 1]
    imag_part = kept[:, 1] - left[:, 0] + right[:, 0]
    return jnp.stack([real_part, imag_part], axis=1).astype(jnp.bfloat16)


def rotate_step(state, prop_re, prop_im):
    state_f = state.astype(jnp.float32)
    real_u = prop_re.astype(jnp.float32)
    imag_u = prop_im.astype(jnp.float32)
    times_re = jnp.einsum('jxab,bc->jxac', state_f, real_u)
    times_im = jnp.einsum('jxab,bc->jxac', state_f, imag_u)
    middle = jnp.stack([times_re[:, 0] - times_im[:, 1], times_im[:, 0] + times_re[:, 1]], axis=1)
    middle = middle.astype(jnp.bfloat16).astype(jnp.float32)
    left_re = jnp.einsum('ba,jxbc->jxac', real_u, middle)
    left_im = jnp.einsum('ba,jxbc->jxac', imag_u, middle)
    result = jnp.stack([left_re[:, 0] + left_im[:, 1], left_re[:, 1] - left_im[:, 0]], axis=1)
    return result.astype(jnp.bfloat16)


def projection(saved_block, state):
    saved_f = saved_block.astype(jnp.float32)
    state_f = state.astype(jnp.float32)
    swapped = jnp.stack([state_f[:, 1], -state_f[:, 0]], axis=1)
    real_part = jnp.einsum('jxba,jxbc->ac', saved_f, state_f)
    imag_part = jnp.einsum('jxba,jxbc->ac', saved_f, swapped)
    return jnp.stack([real_part, imag_part], axis=1)


def reference(adjoint, saved, propagators, coupling, higher, lower, ladder, rates, decay):
    state = adjoint
    columns = []
    for step_index in range(STEPS):
        state_full = state.astype(jnp.float32)
        up_sum = linked_sum(state_full, higher, ladder[0], rates[0])
        down_sum = linked_sum(state_full, lower, ladder[1], rates[1])
        state = couple_step(state, up_sum, down_sum, coupling, decay)
        for substep in range(NSUB):
            state = rotate_step(state, propagators[step_index, substep, 0], propagators[step_index, substep, 1])
            columns.append(projection(saved[step_index, substep], state))
    return state, jnp.stack(columns, axis=1)
```

```python
import jax
import jax.numpy as jnp
from jax import lax
from jax.sharding import PartitionSpec as P


def send_slots(link_table, owners, own_index, own_count, links, capacity):
    flattened = link_table.reshape(owners, links)
    source = flattened // own_count
    local = flattened % own_count
    mine = (source == own_index).astype(jnp.int32)
    before = jnp.cumsum(mine, axis=1) - mine
    picked = [jnp.sum(jnp.where((mine == 1) & (before == 0), local, 0), axis=1)]
    return jnp.stack(picked, axis=1).reshape(owners * capacity)


def receive_slots(link_table, own_index, own_count, links, capacity):
    own_rows = lax.dynamic_slice_in_dim(link_table, own_index * own_count, own_count, 0).reshape(
        links
    )
    source = own_rows // own_count
    positions = jnp.arange(links)
    earlier = (source[:, None] == source[None, :]) & (positions[None, :] < positions[:, None])
    before = jnp.sum(earlier.astype(jnp.int32), axis=1)
    return source * capacity + before


def linked_sum(received, picks, weights, strengths, own_count, modes):
    chosen = received[picks].reshape((own_count, modes) + received.shape[1:])
    factors = weights.astype(jnp.float32) * strengths[None, :]
    total = factors[:, 0, None, None, None] * chosen[:, 0].astype(jnp.float32)
    for mode_index in range(1, modes):
        total = total + factors[:, mode_index, None, None, None] * chosen[:, mode_index].astype(
            jnp.float32
        )
    return total


def couple_step(state, up_sum, down_sum, coupling, decay):
    plus = (up_sum + down_sum).astype(jnp.bfloat16)
    minus = (up_sum - down_sum).astype(jnp.bfloat16)
    left = jnp.einsum("ab,jxbc->jxac", coupling, plus, preferred_element_type=jnp.float32)
    right = jnp.einsum("jxab,bc->jxac", minus, coupling, preferred_element_type=jnp.float32)
    kept = decay[:, None, None, None] * state.astype(jnp.float32)
    real_part = kept[:, 0] + left[:, 1] - right[:, 1]
    imag_part = kept[:, 1] - left[:, 0] + right[:, 0]
    return jnp.stack([real_part, imag_part], axis=1).astype(jnp.bfloat16)


def rotate_step(state, prop_re, prop_im):
    times_re = jnp.einsum("jxab,bc->jxac", state, prop_re, preferred_element_type=jnp.float32)
    times_im = jnp.einsum("jxab,bc->jxac", state, prop_im, preferred_element_type=jnp.float32)
    middle = jnp.stack(
        [times_re[:, 0] - times_im[:, 1], times_im[:, 0] + times_re[:, 1]], axis=1
    ).astype(jnp.bfloat16)
    left_re = jnp.einsum("ba,jxbc->jxac", prop_re, middle, preferred_element_type=jnp.float32)
    left_im = jnp.einsum("ba,jxbc->jxac", prop_im, middle, preferred_element_type=jnp.float32)
    result = jnp.stack([left_re[:, 0] + left_im[:, 1], left_re[:, 1] - left_im[:, 0]], axis=1)
    return result.astype(jnp.bfloat16)


def projection(saved_block, state):
    swapped = jnp.stack([state[:, 1], -state[:, 0]], axis=1)
    real_part = jnp.einsum("jxba,jxbc->ac", saved_block, state, preferred_element_type=jnp.float32)
    imag_part = jnp.einsum(
        "jxba,jxbc->ac", saved_block, swapped, preferred_element_type=jnp.float32
    )
    return jnp.stack([real_part, imag_part], axis=1)


def body(adjoint, saved, propagators, coupling, higher, lower, ladder, rates, decay):
    owners = lax.axis_size(("node", "cores"))
    own_index = lax.axis_index(("node", "cores"))
    own_count = adjoint.shape[0]
    modes = higher.shape[1]
    links = own_count * modes
    capacity = max(1, links // owners)
    step_count = propagators.shape[0]
    sub_count = propagators.shape[1]
    grad_rows = coupling.shape[0] // owners
    up_send = send_slots(higher, owners, own_index, own_count, links, capacity)
    down_send = send_slots(lower, owners, own_index, own_count, links, capacity)
    up_take = receive_slots(higher, own_index, own_count, links, capacity)
    down_take = receive_slots(lower, own_index, own_count, links, capacity)
    state = adjoint
    pieces = []
    for step_index in range(step_count):
        up_out = state[up_send]
        down_out = state[down_send]
        up_in, down_in = (
            lax.all_to_all(up_out, ("node", "cores"), split_axis=0, concat_axis=0, tiled=True),
            lax.all_to_all(down_out, ("node", "cores"), split_axis=0, concat_axis=0, tiled=True),
        )
        up_sum = linked_sum(up_in, up_take, ladder[0], rates[0], own_count, modes)
        down_sum = linked_sum(down_in, down_take, ladder[1], rates[1], own_count, modes)
        state = couple_step(state, up_sum, down_sum, coupling, decay)
        step_terms = []
        for substep in range(sub_count):
            state = rotate_step(
                state, propagators[step_index, substep, 0], propagators[step_index, substep, 1]
            )
            step_terms.append(projection(saved[step_index, substep], state))
        terms = jnp.stack(step_terms, axis=1).astype(jnp.bfloat16)
        swapped = lax.all_to_all(
            terms, ("node", "cores"), split_axis=0, concat_axis=0, tiled=True
        )
        by_owner = swapped.reshape((owners, grad_rows) + swapped.shape[1:])
        pieces.append(jnp.sum(by_owner.astype(jnp.float32), axis=0))
    gradient = jnp.concatenate(pieces, axis=1)
    return (state, gradient)


def solution(mesh):
    return jax.shard_map(
        body,
        mesh=mesh,
        in_specs=(
            P(("node", "cores"), None, None, None),
            P(None, None, ("node", "cores"), None, None, None),
            P(),
            P(),
            P(),
            P(),
            P(None, ("node", "cores"), None),
            P(),
            P(("node", "cores")),
        ),
        out_specs=(P(("node", "cores"), None, None, None), P(("node", "cores"), None, None, None)),
        check_vma=False,
    )
```

```python
import functools

import jax
import jax.numpy as jnp
from jax import lax
from jax.experimental import pallas as pl
from jax.experimental.pallas import tpu as pltpu
from jax.sharding import PartitionSpec as P

MESH = pl.DeviceIdType.MESH
F32 = jnp.float32
BF16 = jnp.bfloat16


def dot(a, b):
    return jnp.dot(a, b, preferred_element_type=F32)


def kernel(
    dims,
    picks,
    takes,
    weights,
    decay,
    adjoint,
    saved,
    propagators,
    coupling,
    out,
    terms,
    right_u,
    left_u,
    hist,
    stage,
    inbox,
    *rest,
):
    nodes, depth, width, count, modes, steps, subs, dim = dims
    hops = depth - 1
    chain = rest[: 2 * steps * hops]
    chain_send, chain_recv, plane_send, plane_recv, credit = rest[2 * steps * hops :]
    cores = depth * width
    owners = nodes * cores
    lanes = nodes * width
    node = lax.axis_index("node")
    spot = lax.axis_index("cores")
    level = spot // width
    column = spot % width
    lane = node * width + column

    def lane_of(offset):
        return lax.rem(lane + offset, lanes)

    def lane_id(other):
        return (other // width, level * width + other % width)

    def level_id(other):
        return (node, other * width + column)

    def owner_of(a_lane, a_level):
        return (a_lane // width) * cores + a_level * width + a_lane % width

    barrier = pltpu.get_barrier_semaphore()

    def greet(offset, carry):
        pl.semaphore_signal(
            barrier, inc=1, device_id=lane_id(lane_of(offset)), device_id_type=MESH
        )
        return carry

    lax.fori_loop(1, lanes, greet, 0)

    @pl.when(level > 0)
    def _():
        pl.semaphore_signal(barrier, inc=1, device_id=level_id(level - 1), device_id_type=MESH)

    @pl.when(level < depth - 1)
    def _():
        pl.semaphore_signal(barrier, inc=1, device_id=level_id(level + 1), device_id_type=MESH)

    inner = jnp.where(level > 0, 1, 0) + jnp.where(level < depth - 1, 1, 0)
    pl.semaphore_wait(barrier, lanes - 1 + inner)

    def chain_block(step, way, hop):
        return chain[(step * 2 + way) * hops + hop - 1]

    def chain_copy(step, way, hop, source):
        peer = level + 1 if way == 0 else level - 1
        return pltpu.make_async_remote_copy(
            src_ref=source,
            dst_ref=chain_block(step, way, hop),
            send_sem=chain_send.at[step, way, hop - 1],
            recv_sem=chain_recv.at[step, way, hop - 1],
            device_id=level_id(peer),
            device_id_type=MESH,
        )

    def from_level(way, hop):
        return level - hop if way == 0 else level + hop

    def arrives(way, hop):
        return level >= hop if way == 0 else level + hop < depth

    def goes_on(way, hop):
        if way == 0:
            return jnp.logical_and(level >= hop - 1, level < depth - 1)
        return jnp.logical_and(level + hop - 1 < depth, level > 0)

    def plane_copy(offset, a_level):
        return pltpu.make_async_remote_copy(
            src_ref=stage.at[offset - 1, a_level],
            dst_ref=inbox.at[owner_of(lane, a_level)],
            send_sem=plane_send.at[offset - 1, a_level],
            recv_sem=plane_recv.at[owner_of(lane, a_level)],
            device_id=lane_id(lane_of(offset)),
            device_id_type=MESH,
        )

    def serve(block, a_level):
        source = owner_of(lane, a_level)

        def pick(offset, way):
            target = owner_of(lane_of(offset), level)
            return picks[(way * owners + target) * owners + source]

        for way in range(2):
            inbox[source, way] = block[pick(0, way)]

        def fill(offset, carry):
            for way in range(2):
                stage[offset - 1, a_level, way] = block[pick(offset, way)]
            return carry

        lax.fori_loop(1, lanes, fill, 0)

        def send(offset, carry):
            plane_copy(offset, a_level).start()
            return carry

        lax.fori_loop(1, lanes, send, 0)

    def prepare():
        def one(at, carry):
            step, sub = at // subs, at % subs
            u_re = propagators[step, sub, 0]
            u_im = propagators[step, sub, 1]
            right_u[at, :dim, :dim] = u_re
            right_u[at, :dim, dim:] = u_im
            right_u[at, dim:, :dim] = -u_im
            right_u[at, dim:, dim:] = u_re
            t_re = u_re.T
            t_im = u_im.T
            left_u[at, :dim, :dim] = t_re
            left_u[at, :dim, dim:] = t_im
            left_u[at, dim:, :dim] = -t_im
            left_u[at, dim:, dim:] = t_re
            return carry

        lax.fori_loop(0, steps * subs, one, 0)

    def project(step):
        def one(sub, carry):
            total = jnp.zeros((dim, 2 * dim), F32)
            for j in range(count):
                kept = saved[step, sub, j].reshape(2 * dim, dim)
                lam_re = hist[step, sub + 1, j, 0]
                lam_im = hist[step, sub + 1, j, 1]
                both = jnp.concatenate(
                    [
                        jnp.concatenate([lam_re, lam_im], axis=1),
                        jnp.concatenate([lam_im, -lam_re], axis=1),
                    ],
                    axis=0,
                )
                total = total + lax.dot_general(
                    kept, both, (((0,), (0,)), ((), ())), preferred_element_type=F32
                )
            terms[step * subs + sub] = total.astype(BF16)
            return carry

        lax.fori_loop(0, subs, one, 0)

    def couple(step, state):
        operator = coupling[...]

        def one(j, carry):
            plus, minus = [], []
            for part in range(2):
                sums = []
                for way in range(2):
                    total = jnp.zeros((dim, dim), F32)
                    for mode in range(modes):
                        at = (way * count + j) * modes + mode
                        total = total + weights[at] * inbox[takes[at], way, part].astype(F32)
                    sums.append(total)
                plus.append((sums[0] + sums[1]).astype(BF16))
                minus.append((sums[0] - sums[1]).astype(BF16))
            left = dot(operator, jnp.concatenate([plus[1], -plus[0]], axis=1))
            right = dot(jnp.concatenate([minus[1], -minus[0]], axis=0), operator)
            for part in range(2):
                lam = decay[j] * state[j, part].astype(F32)
                lam = lam + left[:, part * dim : (part + 1) * dim]
                lam = lam - right[part * dim : (part + 1) * dim]
                hist[step, 0, j, part] = lam.astype(BF16)
            return carry

        lax.fori_loop(0, count, one, 0)

    def rotate(step):
        def one(sub, carry):
            at = step * subs + sub
            mult_r = right_u[at]
            mult_l = left_u[at]
            for j in range(0, count, 2):
                rows = jnp.concatenate(
                    [
                        jnp.concatenate(
                            [hist[step, sub, j + i, 0], hist[step, sub, j + i, 1]], axis=1
                        )
                        for i in range(2)
                    ],
                    axis=0,
                )
                middle = dot(rows, mult_r).astype(BF16)
                stacked = jnp.concatenate(
                    [
                        jnp.concatenate([middle[:dim, :dim], middle[dim:, :dim]], axis=1),
                        jnp.concatenate([middle[:dim, dim:], middle[dim:, dim:]], axis=1),
                    ],
                    axis=0,
                )
                result = dot(mult_l, stacked).astype(BF16)
                for i in range(2):
                    for part in range(2):
                        hist[step, sub + 1, j + i, part] = result[
                            part * dim : (part + 1) * dim, i * dim : (i + 1) * dim
                        ]
            return carry

        lax.fori_loop(0, subs, one, 0)

    for step in range(steps):
        state = adjoint if step == 0 else hist.at[step - 1, subs]
        for way in range(2):

            @pl.when(goes_on(way, 1))
            def _(way=way):
                chain_copy(step, way, 1, state).start()

        if step > 0:
            pl.semaphore_wait(credit, lanes - 1)
        serve(state, level)
        if step == 0:
            prepare()
        else:
            project(step - 1)
        for hop in range(1, depth):
            for way in range(2):

                @pl.when(arrives(way, hop))
                def _(way=way, hop=hop):
                    block = chain_block(step, way, hop)
                    chain_copy(step, way, hop, block).wait_recv()
                    if hop + 1 < depth:

                        @pl.when(goes_on(way, hop + 1))
                        def _():
                            chain_copy(step, way, hop + 1, block).start()

                    serve(block, from_level(way, hop))

        def collect(offset, carry):
            for a_level in range(depth):
                source = owner_of(lane_of(offset), a_level)
                pltpu.make_async_remote_copy(
                    src_ref=stage.at[offset - 1, a_level],
                    dst_ref=inbox.at[source],
                    send_sem=plane_send.at[offset - 1, a_level],
                    recv_sem=plane_recv.at[source],
                    device_id=lane_id(lane_of(offset)),
                    device_id_type=MESH,
                ).wait_recv()
            return carry

        lax.fori_loop(1, lanes, collect, 0)
        couple(step, state)
        if step + 1 < steps:

            def allow(offset, carry):
                pl.semaphore_signal(
                    credit, inc=1, device_id=lane_id(lane_of(offset)), device_id_type=MESH
                )
                return carry

            lax.fori_loop(1, lanes, allow, 0)
        rotate(step)

        def settle(offset, carry):
            for a_level in range(depth):
                plane_copy(offset, a_level).wait_send()
            return carry

        lax.fori_loop(1, lanes, settle, 0)
        for hop in range(1, depth):
            for way in range(2):

                @pl.when(goes_on(way, hop))
                def _(way=way, hop=hop):
                    chain_copy(step, way, hop, chain_block(step, way, hop)).wait_send()

    out[...] = hist[steps - 1, subs]
    project(steps - 1)


def pick_table(links, owners, count):
    flat = links.reshape(owners, -1)
    hit = (flat // count)[:, None, :] == jnp.arange(owners)[None, :, None]
    return jnp.sum(jnp.where(hit, (flat % count)[:, None, :], 0), axis=2).reshape(-1)


def body(adjoint, saved, propagators, coupling, higher, lower, ladder, rates, decay):
    nodes = lax.axis_size("node")
    cores = lax.axis_size("cores")
    owners = nodes * cores
    own = lax.axis_index(("node", "cores"))
    count = adjoint.shape[0]
    modes = higher.shape[1]
    steps, subs = propagators.shape[:2]
    dim = coupling.shape[0]
    depth = 1 << (cores.bit_length() // 2)
    width = cores // depth
    lanes = nodes * width
    grad_rows = dim // owners if dim >= owners else 1
    picks = jnp.concatenate(
        [pick_table(higher, owners, count), pick_table(lower, owners, count)]
    ).astype(jnp.int32)
    own_links = lax.dynamic_slice_in_dim(jnp.stack([higher, lower]), own * count, count, 1)
    takes = (own_links // count).reshape(-1).astype(jnp.int32)
    weights = (ladder.astype(F32) * rates[:, None, :]).reshape(-1)
    block = adjoint.shape
    smem = pl.BlockSpec(memory_space=pltpu.SMEM)
    vmem = pl.BlockSpec(memory_space=pltpu.VMEM)
    hops = depth - 1
    state, terms = pl.pallas_call(
        functools.partial(kernel, (nodes, depth, width, count, modes, steps, subs, dim)),
        out_shape=(
            jax.ShapeDtypeStruct(block, BF16),
            jax.ShapeDtypeStruct((steps * subs, dim, 2 * dim), BF16),
        ),
        in_specs=[smem] * 4 + [vmem] * 4,
        out_specs=(vmem, vmem),
        scratch_shapes=[
            pltpu.VMEM((steps * subs, 2 * dim, 2 * dim), BF16),
            pltpu.VMEM((steps * subs, 2 * dim, 2 * dim), BF16),
            pltpu.VMEM((steps, subs + 1) + block, BF16),
            pltpu.VMEM((lanes - 1, depth, 2) + block[1:], BF16),
            pltpu.VMEM((owners, 2) + block[1:], BF16),
            *[pltpu.VMEM(block, BF16) for _ in range(2 * steps * hops)],
            pltpu.SemaphoreType.DMA((steps, 2, hops)),
            pltpu.SemaphoreType.DMA((steps, 2, hops)),
            pltpu.SemaphoreType.DMA((lanes - 1, depth)),
            pltpu.SemaphoreType.DMA((owners,)),
            pltpu.SemaphoreType.REGULAR,
        ],
        compiler_params=pltpu.CompilerParams(
            collective_id=0, has_side_effects=True, vmem_limit_bytes=63_000_000
        ),
    )(picks, takes, weights, decay, adjoint, saved, propagators, coupling)
    swapped = lax.all_to_all(
        jnp.swapaxes(terms, 0, 1), ("node", "cores"), split_axis=0, concat_axis=0, tiled=True
    )
    by_owner = swapped.reshape(owners, grad_rows, steps * subs, 2, dim)
    gradient = jnp.sum(by_owner.astype(F32), axis=0)
    return state, gradient


def solution(mesh):
    return jax.shard_map(
        body,
        mesh=mesh,
        in_specs=(
            P(("node", "cores"), None, None, None),
            P(None, None, ("node", "cores"), None, None, None),
            P(),
            P(),
            P(),
            P(),
            P(None, ("node", "cores"), None),
            P(),
            P(("node", "cores")),
        ),
        out_specs=(P(("node", "cores"), None, None, None), P(("node", "cores"), None, None, None)),
        check_vma=False,
    )
```

```python
import functools

import jax
import jax.numpy as jnp
from jax import lax
from jax.experimental import pallas as pl
from jax.experimental.pallas import tpu as pltpu
from jax.sharding import PartitionSpec as P

MESH = pl.DeviceIdType.MESH
F32 = jnp.float32
BF16 = jnp.bfloat16


def dot(a, b):
    return jnp.dot(a, b, preferred_element_type=F32)


def kernel(
    dims,
    picks,
    higher,
    lower,
    ladder,
    rates,
    decay,
    adjoint,
    saved,
    propagators,
    coupling,
    out,
    grad,
    right_u,
    left_u,
    hist,
    stage,
    inbox,
    terms,
    term_stage,
    term_inbox,
    *rest,
):
    nodes, depth, width, count, modes, steps, subs, dim, halves = dims
    hops = depth - 1
    chain = rest[: 2 * steps * hops]
    chain_send, chain_recv, plane_send, plane_recv, term_send, term_recv, credit = rest[
        2 * steps * hops :
    ]
    cores = depth * width
    owners = nodes * cores
    lanes = nodes * width
    rows = dim // owners
    batch = subs // halves
    node = lax.axis_index("node")
    spot = lax.axis_index("cores")
    level = spot // width
    column = spot % width
    lane = node * width + column

    def lane_of(offset):
        return lax.rem(lane + offset, lanes)

    def lane_id(other):
        return (other // width, level * width + other % width)

    def level_id(other):
        return (node, other * width + column)

    def owner_of(a_lane, a_level):
        return (a_lane // width) * cores + a_level * width + a_lane % width

    barrier = pltpu.get_barrier_semaphore()

    own = node * cores + spot

    def owner_id(offset):
        other = lax.rem(own + offset, owners)
        return (other // cores, lax.rem(other, cores))

    def greet(offset, carry):
        pl.semaphore_signal(barrier, inc=1, device_id=owner_id(offset), device_id_type=MESH)
        return carry

    lax.fori_loop(1, owners, greet, 0)
    pl.semaphore_wait(barrier, owners - 1)

    def chain_block(step, way, hop):
        return chain[(step * 2 + way) * hops + hop - 1]

    def chain_copy(step, way, hop, source):
        peer = level + 1 if way == 0 else level - 1
        return pltpu.make_async_remote_copy(
            src_ref=source,
            dst_ref=chain_block(step, way, hop),
            send_sem=chain_send.at[step, way, hop - 1],
            recv_sem=chain_recv.at[step, way, hop - 1],
            device_id=level_id(peer),
            device_id_type=MESH,
        )

    def from_level(way, hop):
        return level - hop if way == 0 else level + hop

    def arrives(way, hop):
        return level >= hop if way == 0 else level + hop < depth

    def goes_on(way, hop):
        if way == 0:
            return jnp.logical_and(level >= hop - 1, level < depth - 1)
        return jnp.logical_and(level + hop - 1 < depth, level > 0)

    def plane_copy(offset, a_level):
        return pltpu.make_async_remote_copy(
            src_ref=stage.at[offset - 1, a_level],
            dst_ref=inbox.at[owner_of(lane, a_level)],
            send_sem=plane_send.at[offset - 1, a_level],
            recv_sem=plane_recv.at[owner_of(lane, a_level)],
            device_id=lane_id(lane_of(offset)),
            device_id_type=MESH,
        )

    def serve(block, a_level):
        source = owner_of(lane, a_level)

        def pick(offset, way):
            target = owner_of(lane_of(offset), level)
            return picks[way * owners + source, target]

        for way in range(2):
            inbox[source, way] = block[pick(0, way)]

        def fill(offset, carry):
            for way in range(2):
                stage[offset - 1, a_level, way] = block[pick(offset, way)]
            return carry

        lax.fori_loop(1, lanes, fill, 0)

        def send(offset, carry):
            plane_copy(offset, a_level).start()
            return carry

        lax.fori_loop(1, lanes, send, 0)

    def prepare():
        def one(at, carry):
            step, sub = at // subs, at % subs
            u_re = propagators[step, sub, 0]
            u_im = propagators[step, sub, 1]
            right_u[at, :dim, :dim] = u_re
            right_u[at, :dim, dim:] = u_im
            right_u[at, dim:, :dim] = -u_im
            right_u[at, dim:, dim:] = u_re
            t_re = u_re.T
            t_im = u_im.T
            left_u[at, :dim, :dim] = t_re
            left_u[at, :dim, dim:] = t_im
            left_u[at, dim:, :dim] = -t_im
            left_u[at, dim:, dim:] = t_re
            return carry

        lax.fori_loop(0, steps * subs, one, 0)

    def project(step, half):
        group = step * halves + half

        def one(place, carry):
            sub = half * batch + place
            total = jnp.zeros((dim, 2 * dim), F32)
            for j in range(count):
                kept = saved[step, sub, j].reshape(2 * dim, dim)
                lam_re = hist[step, sub + 1, j, 0]
                lam_im = hist[step, sub + 1, j, 1]
                both = jnp.concatenate(
                    [
                        jnp.concatenate([lam_re, lam_im], axis=1),
                        jnp.concatenate([lam_im, -lam_re], axis=1),
                    ],
                    axis=0,
                )
                total = total + lax.dot_general(
                    kept, both, (((0,), (0,)), ((), ())), preferred_element_type=F32
                )
            terms[place] = total
            return carry

        lax.fori_loop(0, batch, one, 0)
        for target in range(owners):
            term_stage[group, target] = jnp.concatenate(
                [terms[i, target * rows : (target + 1) * rows] for i in range(batch)], axis=0
            ).astype(BF16)

        def send(offset, carry):
            pltpu.make_async_remote_copy(
                src_ref=term_stage.at[group, lax.rem(own + offset, owners)],
                dst_ref=term_inbox.at[group, offset - 1],
                send_sem=term_send.at[group],
                recv_sem=term_recv.at[group],
                device_id=owner_id(offset),
                device_id_type=MESH,
            ).start()
            return carry

        lax.fori_loop(1, owners, send, 0)

    def finish(group):
        everything = term_inbox.at[group]
        pltpu.make_async_copy(everything, everything, term_recv.at[group]).wait()
        total = term_stage[group, own].astype(F32)
        for offset in range(1, owners):
            total = total + term_inbox[group, offset - 1].astype(F32)
        for i in range(batch):
            grad[group * batch + i] = total[i * rows : (i + 1) * rows]
        pltpu.make_async_copy(everything, everything, term_send.at[group]).wait()

    def couple(step, state):
        operator = coupling[...]

        def one(j, carry):
            plus, minus = [], []
            for part in range(2):
                sums = []
                for way in range(2):
                    total = jnp.zeros((dim, dim), F32)
                    for mode in range(modes):
                        weight = ladder[way, mode, j].astype(F32) * rates[way, mode]
                        place = lax.div((higher, lower)[way][mode, own * count + j], count)
                        total = total + weight * inbox[place, way, part].astype(F32)
                    sums.append(total)
                plus.append((sums[0] + sums[1]).astype(BF16))
                minus.append((sums[0] - sums[1]).astype(BF16))
            left = dot(operator, jnp.concatenate([plus[1], -plus[0]], axis=1))
            right = dot(jnp.concatenate([minus[1], -minus[0]], axis=0), operator)
            for part in range(2):
                lam = decay[j] * state[j, part].astype(F32)
                lam = lam + left[:, part * dim : (part + 1) * dim]
                lam = lam - right[part * dim : (part + 1) * dim]
                hist[step, 0, j, part] = lam.astype(BF16)
            return carry

        lax.fori_loop(0, count, one, 0)

    def rotate(step, half):
        def one(sub, carry):
            at = step * subs + sub
            mult_r = right_u[at]
            mult_l = left_u[at]
            for j in range(0, count, 2):
                rows = jnp.concatenate(
                    [
                        jnp.concatenate(
                            [hist[step, sub, j + i, 0], hist[step, sub, j + i, 1]], axis=1
                        )
                        for i in range(2)
                    ],
                    axis=0,
                )
                middle = dot(rows, mult_r).astype(BF16)
                stacked = jnp.concatenate(
                    [
                        jnp.concatenate([middle[:dim, :dim], middle[dim:, :dim]], axis=1),
                        jnp.concatenate([middle[:dim, dim:], middle[dim:, dim:]], axis=1),
                    ],
                    axis=0,
                )
                result = dot(mult_l, stacked).astype(BF16)
                for i in range(2):
                    for part in range(2):
                        hist[step, sub + 1, j + i, part] = result[
                            part * dim : (part + 1) * dim, i * dim : (i + 1) * dim
                        ]
            return carry

        lax.fori_loop(half * batch, (half + 1) * batch, one, 0)

    for step in range(steps):
        state = adjoint if step == 0 else hist.at[step - 1, subs]
        for way in range(2):

            @pl.when(goes_on(way, 1))
            def _(way=way):
                chain_copy(step, way, 1, state).start()

        if step > 0:
            pl.semaphore_wait(credit, lanes - 1)
        serve(state, level)
        if step == 0:
            prepare()
        else:
            for half in range(halves):
                project(step - 1, half)
        for hop in range(1, depth):
            for way in range(2):

                @pl.when(arrives(way, hop))
                def _(way=way, hop=hop):
                    block = chain_block(step, way, hop)
                    chain_copy(step, way, hop, block).wait_recv()
                    if hop + 1 < depth:

                        @pl.when(goes_on(way, hop + 1))
                        def _():
                            chain_copy(step, way, hop + 1, block).start()

                    serve(block, from_level(way, hop))

        def collect(offset, carry):
            for a_level in range(depth):
                source = owner_of(lane_of(offset), a_level)
                pltpu.make_async_remote_copy(
                    src_ref=stage.at[offset - 1, a_level],
                    dst_ref=inbox.at[source],
                    send_sem=plane_send.at[offset - 1, a_level],
                    recv_sem=plane_recv.at[source],
                    device_id=lane_id(lane_of(offset)),
                    device_id_type=MESH,
                ).wait_recv()
            return carry

        lax.fori_loop(1, lanes, collect, 0)
        couple(step, state)
        if step + 1 < steps:

            def allow(offset, carry):
                pl.semaphore_signal(
                    credit, inc=1, device_id=lane_id(lane_of(offset)), device_id_type=MESH
                )
                return carry

            lax.fori_loop(1, lanes, allow, 0)
        for half in range(halves):
            rotate(step, half)
            if step == steps - 1:
                project(step, half)

        def settle(offset, carry):
            for a_level in range(depth):
                plane_copy(offset, a_level).wait_send()
            return carry

        lax.fori_loop(1, lanes, settle, 0)
        for hop in range(1, depth):
            for way in range(2):

                @pl.when(goes_on(way, hop))
                def _(way=way, hop=hop):
                    chain_copy(step, way, hop, chain_block(step, way, hop)).wait_send()

    out[...] = hist[steps - 1, subs]
    for group in range(steps * halves):
        finish(group)


def pick_kernel(owners, count, modes, higher, lower, picks):
    total = owners * count
    names = lax.broadcasted_iota(jnp.int32, (owners, total), 0)
    member = lax.div(lax.broadcasted_iota(jnp.int32, (total, owners), 0), count)
    member = (member == lax.broadcasted_iota(jnp.int32, (total, owners), 1)).astype(F32)
    for way, table in enumerate((higher, lower)):
        spread = jnp.zeros((owners, total), F32)
        for mode in range(modes):
            link = table[mode : mode + 1, :]
            source = lax.div(link, count)
            local = (link - source * count).astype(F32)
            spread = spread + jnp.where(source == names, local, 0.0)
        found = dot(spread.astype(BF16), member.astype(BF16))
        picks[way * owners : (way + 1) * owners, :] = found.astype(jnp.int32)


def body(adjoint, saved, propagators, coupling, higher, lower, ladder, rates, decay):
    nodes = lax.axis_size("node")
    cores = lax.axis_size("cores")
    owners = nodes * cores
    own = lax.axis_index(("node", "cores"))
    count = adjoint.shape[0]
    modes = higher.shape[1]
    steps, subs = propagators.shape[:2]
    dim = coupling.shape[0]
    depth = 1 << (cores.bit_length() // 2)
    width = cores // depth
    lanes = nodes * width
    rows = dim // owners
    halves = 2 if subs % 2 == 0 else 1
    batch = subs // halves
    higher, lower, ladder = higher.T, lower.T, jnp.swapaxes(ladder, 1, 2)
    smem = pl.BlockSpec(memory_space=pltpu.SMEM)
    vmem = pl.BlockSpec(memory_space=pltpu.VMEM)
    picks = pl.pallas_call(
        functools.partial(pick_kernel, owners, count, modes),
        out_shape=jax.ShapeDtypeStruct((2 * owners, owners), jnp.int32),
        in_specs=[vmem, vmem],
        out_specs=vmem,
    )(higher, lower)
    block = adjoint.shape
    hops = depth - 1
    state, grad = pl.pallas_call(
        functools.partial(kernel, (nodes, depth, width, count, modes, steps, subs, dim, halves)),
        out_shape=(
            jax.ShapeDtypeStruct(block, BF16),
            jax.ShapeDtypeStruct((steps * subs, rows, 2 * dim), F32),
        ),
        in_specs=[smem] * 6 + [vmem] * 4,
        out_specs=(vmem, vmem),
        scratch_shapes=[
            pltpu.VMEM((steps * subs, 2 * dim, 2 * dim), BF16),
            pltpu.VMEM((steps * subs, 2 * dim, 2 * dim), BF16),
            pltpu.VMEM((steps, subs + 1) + block, BF16),
            pltpu.VMEM((lanes - 1, depth, 2) + block[1:], BF16),
            pltpu.VMEM((owners, 2) + block[1:], BF16),
            pltpu.VMEM((batch, dim, 2 * dim), F32),
            pltpu.VMEM((steps * halves, owners, batch * rows, 2 * dim), BF16),
            pltpu.VMEM((steps * halves, owners - 1, batch * rows, 2 * dim), BF16),
            *[pltpu.VMEM(block, BF16) for _ in range(2 * steps * hops)],
            pltpu.SemaphoreType.DMA((steps, 2, hops)),
            pltpu.SemaphoreType.DMA((steps, 2, hops)),
            pltpu.SemaphoreType.DMA((lanes - 1, depth)),
            pltpu.SemaphoreType.DMA((owners,)),
            pltpu.SemaphoreType.DMA((steps * halves,)),
            pltpu.SemaphoreType.DMA((steps * halves,)),
            pltpu.SemaphoreType.REGULAR,
        ],
        compiler_params=pltpu.CompilerParams(
            collective_id=0, has_side_effects=True, vmem_limit_bytes=63_000_000
        ),
    )(picks, higher, lower, ladder, rates, decay, adjoint, saved, propagators, coupling)
    gradient = jnp.swapaxes(grad, 0, 1).reshape(rows, steps * subs, 2, dim)
    return state, gradient


def solution(mesh):
    return jax.shard_map(
        body,
        mesh=mesh,
        in_specs=(
            P(("node", "cores"), None, None, None),
            P(None, None, ("node", "cores"), None, None, None),
            P(),
            P(),
            P(),
            P(),
            P(None, ("node", "cores"), None),
            P(),
            P(("node", "cores")),
        ),
        out_specs=(P(("node", "cores"), None, None, None), P(("node", "cores"), None, None, None)),
        check_vma=False,
    )
```

```python
import functools

import jax
import jax.numpy as jnp
from jax import lax
from jax.experimental import pallas as pl
from jax.experimental.pallas import tpu as pltpu
from jax.sharding import PartitionSpec as P

MESH = pl.DeviceIdType.MESH
F32 = jnp.float32
BF16 = jnp.bfloat16


def dot(a, b):
    return jnp.dot(a, b, preferred_element_type=F32)


def kernel(
    dims,
    picks,
    higher,
    lower,
    ladder,
    rates,
    decay,
    adjoint,
    saved_in,
    propagators,
    coupling,
    out,
    grad,
    right_u,
    left_u,
    hist,
    stage,
    inbox,
    terms,
    term_stage,
    term_inbox,
    saved,
    saved_t,
    *rest,
):
    nodes, depth, width, count, modes, steps, subs, dim, halves = dims
    hops = depth - 1
    chain = rest[: 2 * steps * hops]
    chain_send, chain_recv, plane_send, plane_recv, term_send, term_recv, local, credit = rest[
        2 * steps * hops :
    ]
    cores = depth * width
    owners = nodes * cores
    lanes = nodes * width
    rows = dim // owners
    batch = subs // halves
    node = lax.axis_index("node")
    spot = lax.axis_index("cores")
    level = spot // width
    column = spot % width
    lane = node * width + column

    def lane_of(offset):
        return lax.rem(lane + offset, lanes)

    def lane_id(other):
        return (other // width, level * width + other % width)

    def level_id(other):
        return (node, other * width + column)

    def owner_of(a_lane, a_level):
        return (a_lane // width) * cores + a_level * width + a_lane % width

    barrier = pltpu.get_barrier_semaphore()

    own = node * cores + spot

    def owner_id(offset):
        other = lax.rem(own + offset, owners)
        return (other // cores, lax.rem(other, cores))

    def greet(offset, carry):
        pl.semaphore_signal(barrier, inc=1, device_id=owner_id(offset), device_id_type=MESH)
        return carry

    lax.fori_loop(1, owners, greet, 0)
    fetch = pltpu.make_async_copy(saved_in, saved, local.at[0])
    fetch.start()

    def chain_block(step, way, hop):
        return chain[(step * 2 + way) * hops + hop - 1]

    def chain_copy(step, way, hop, source):
        peer = level + 1 if way == 0 else level - 1
        return pltpu.make_async_remote_copy(
            src_ref=source,
            dst_ref=chain_block(step, way, hop),
            send_sem=chain_send.at[step, way, hop - 1],
            recv_sem=chain_recv.at[step, way, hop - 1],
            device_id=level_id(peer),
            device_id_type=MESH,
        )

    def from_level(way, hop):
        return level - hop if way == 0 else level + hop

    def arrives(way, hop):
        return level >= hop if way == 0 else level + hop < depth

    def goes_on(way, hop):
        if way == 0:
            return jnp.logical_and(level >= hop - 1, level < depth - 1)
        return jnp.logical_and(level + hop - 1 < depth, level > 0)

    def plane_copy(offset, a_level):
        return pltpu.make_async_remote_copy(
            src_ref=stage.at[offset - 1, a_level],
            dst_ref=inbox.at[owner_of(lane, a_level)],
            send_sem=plane_send.at[offset - 1, a_level],
            recv_sem=plane_recv.at[owner_of(lane, a_level)],
            device_id=lane_id(lane_of(offset)),
            device_id_type=MESH,
        )

    def serve(block, a_level):
        fill_stage(block, a_level)
        send_stage(a_level)

    def fill_stage(block, a_level):
        source = owner_of(lane, a_level)

        def pick(offset, way):
            target = owner_of(lane_of(offset), level)
            return picks[way * owners + source, target]

        for way in range(2):
            inbox[source, way] = block[pick(0, way)]

        def fill(offset, carry):
            for way in range(2):
                stage[offset - 1, a_level, way] = block[pick(offset, way)]
            return carry

        lax.fori_loop(1, lanes, fill, 0)

    def send_stage(a_level):
        def send(offset, carry):
            plane_copy(offset, a_level).start()
            return carry

        lax.fori_loop(1, lanes, send, 0)

    def prepare():
        def one(at, carry):
            step, sub = at // subs, at % subs
            u_re = propagators[step, sub, 0]
            u_im = propagators[step, sub, 1]
            right_u[at, :dim, :dim] = u_re
            right_u[at, :dim, dim:] = u_im
            right_u[at, dim:, :dim] = -u_im
            right_u[at, dim:, dim:] = u_re
            t_re = u_re.T
            t_im = u_im.T
            left_u[at, :dim, :dim] = t_re
            left_u[at, :dim, dim:] = t_im
            left_u[at, dim:, :dim] = -t_im
            left_u[at, dim:, dim:] = t_re
            return carry

        lax.fori_loop(0, steps * subs, one, 0)

    def turn(sub):
        for j in range(count):
            kept = saved[steps - 1, sub, j].reshape(2 * dim, dim)
            saved_t[sub, :, 2 * dim * j : 2 * dim * (j + 1)] = kept.T

    def project(step, sub):
        total = jnp.zeros((dim, 2 * dim), F32)
        for j in range(count):
            lam_re = hist[step, sub + 1, j, 0]
            lam_im = hist[step, sub + 1, j, 1]
            both = jnp.concatenate(
                [
                    jnp.concatenate([lam_re, lam_im], axis=1),
                    jnp.concatenate([lam_im, -lam_re], axis=1),
                ],
                axis=0,
            )
            if step == steps - 1:
                kept_t = saved_t[sub, :, 2 * dim * j : 2 * dim * (j + 1)]
                total = total + dot(kept_t, both)
            else:
                kept = saved[step, sub, j].reshape(2 * dim, dim)
                total = total + lax.dot_general(
                    kept, both, (((0,), (0,)), ((), ())), preferred_element_type=F32
                )
        terms[sub % batch] = total
        if sub % batch == batch - 1:
            spread(step * halves + sub // batch)

    def spread(group):
        for target in range(owners):
            term_stage[group, target] = jnp.concatenate(
                [terms[i, target * rows : (target + 1) * rows] for i in range(batch)], axis=0
            ).astype(BF16)

        def send(offset, carry):
            pltpu.make_async_remote_copy(
                src_ref=term_stage.at[group, lax.rem(own + offset, owners)],
                dst_ref=term_inbox.at[group, offset - 1],
                send_sem=term_send.at[group],
                recv_sem=term_recv.at[group],
                device_id=owner_id(offset),
                device_id_type=MESH,
            ).start()
            return carry

        lax.fori_loop(1, owners, send, 0)

    def finish(group):
        everything = term_inbox.at[group]
        pltpu.make_async_copy(everything, everything, term_recv.at[group]).wait()
        total = term_stage[group, own].astype(F32)
        for offset in range(1, owners):
            total = total + term_inbox[group, offset - 1].astype(F32)
        for i in range(batch):
            for row in range(rows):
                for part in range(2):
                    grad[row, group * batch + i, part : part + 1, :] = total[
                        i * rows + row : i * rows + row + 1, part * dim : (part + 1) * dim
                    ]
        pltpu.make_async_copy(everything, everything, term_send.at[group]).wait()

    def couple(step, state):
        operator = coupling[...]

        def one(j, carry):
            plus, minus = [], []
            for part in range(2):
                sums = []
                for way in range(2):
                    total = jnp.zeros((dim, dim), F32)
                    for mode in range(modes):
                        weight = ladder[way, mode, j].astype(F32) * rates[way, mode]
                        place = lax.div((higher, lower)[way][mode, own * count + j], count)
                        total = total + weight * inbox[place, way, part].astype(F32)
                    sums.append(total)
                plus.append((sums[0] + sums[1]).astype(BF16))
                minus.append((sums[0] - sums[1]).astype(BF16))
            left = dot(operator, jnp.concatenate([plus[1], -plus[0]], axis=1))
            right = dot(jnp.concatenate([minus[1], -minus[0]], axis=0), operator)
            for part in range(2):
                lam = decay[j] * state[j, part].astype(F32)
                lam = lam + left[:, part * dim : (part + 1) * dim]
                lam = lam - right[part * dim : (part + 1) * dim]
                hist[step, 0, j, part] = lam.astype(BF16)
            return carry

        lax.fori_loop(0, count, one, 0)

    def rotate(step, half):
        def one(sub, carry):
            at = step * subs + sub
            mult_r = right_u[at]
            mult_l = left_u[at]
            for j in range(0, count, 2):
                rows = jnp.concatenate(
                    [
                        jnp.concatenate(
                            [hist[step, sub, j + i, 0], hist[step, sub, j + i, 1]], axis=1
                        )
                        for i in range(2)
                    ],
                    axis=0,
                )
                middle = dot(rows, mult_r).astype(BF16)
                stacked = jnp.concatenate(
                    [
                        jnp.concatenate([middle[:dim, :dim], middle[dim:, :dim]], axis=1),
                        jnp.concatenate([middle[:dim, dim:], middle[dim:, dim:]], axis=1),
                    ],
                    axis=0,
                )
                result = dot(mult_l, stacked).astype(BF16)
                for i in range(2):
                    for part in range(2):
                        hist[step, sub + 1, j + i, part] = result[
                            part * dim : (part + 1) * dim, i * dim : (i + 1) * dim
                        ]
            return carry

        lax.fori_loop(half * batch, (half + 1) * batch, one, 0)

    prepare()
    fill_stage(adjoint, level)
    pl.semaphore_wait(barrier, owners - 1)
    for step in range(steps):
        state = adjoint if step == 0 else hist.at[step - 1, subs]
        for way in range(2):

            @pl.when(goes_on(way, 1))
            def _(way=way):
                chain_copy(step, way, 1, state).start()

        if step > 0:
            pl.semaphore_wait(credit, lanes - 1)
            fill_stage(state, level)
        send_stage(level)
        if step == 0:
            fetch.wait()
        beside = [[] for _ in range(depth)]
        for sub in range(subs):
            beside[sub * depth // subs].append(sub)

        def aside(place):
            for sub in beside[place]:
                if step > 0:
                    project(step - 1, sub)
                if step == 0:
                    turn(sub)

        aside(0)
        for hop in range(1, depth):
            for way in range(2):

                @pl.when(arrives(way, hop))
                def _(way=way, hop=hop):
                    block = chain_block(step, way, hop)
                    chain_copy(step, way, hop, block).wait_recv()
                    if hop + 1 < depth:

                        @pl.when(goes_on(way, hop + 1))
                        def _():
                            chain_copy(step, way, hop + 1, block).start()

                    serve(block, from_level(way, hop))

            aside(hop)

        def collect(offset, carry):
            for a_level in range(depth):
                source = owner_of(lane_of(offset), a_level)
                pltpu.make_async_remote_copy(
                    src_ref=stage.at[offset - 1, a_level],
                    dst_ref=inbox.at[source],
                    send_sem=plane_send.at[offset - 1, a_level],
                    recv_sem=plane_recv.at[source],
                    device_id=lane_id(lane_of(offset)),
                    device_id_type=MESH,
                ).wait_recv()
            return carry

        lax.fori_loop(1, lanes, collect, 0)
        couple(step, state)
        if step + 1 < steps:

            def allow(offset, carry):
                pl.semaphore_signal(
                    credit, inc=1, device_id=lane_id(lane_of(offset)), device_id_type=MESH
                )
                return carry

            lax.fori_loop(1, lanes, allow, 0)
        for half in range(halves):
            rotate(step, half)
            if step == steps - 1:
                for sub in range(half * batch, (half + 1) * batch):
                    project(step, sub)
                    if sub == subs - 1:
                        result = pltpu.make_async_copy(hist.at[step, subs], out, local.at[1])
                        result.start()

        def settle(offset, carry):
            for a_level in range(depth):
                plane_copy(offset, a_level).wait_send()
            return carry

        lax.fori_loop(1, lanes, settle, 0)
        for hop in range(1, depth):
            for way in range(2):

                @pl.when(goes_on(way, hop))
                def _(way=way, hop=hop):
                    chain_copy(step, way, hop, chain_block(step, way, hop)).wait_send()

    result.wait()
    for group in range(steps * halves):
        finish(group)


def pick_kernel(owners, count, modes, higher, lower, picks):
    total = owners * count
    names = lax.broadcasted_iota(jnp.int32, (owners, total), 0)
    member = lax.div(lax.broadcasted_iota(jnp.int32, (total, owners), 0), count)
    member = (member == lax.broadcasted_iota(jnp.int32, (total, owners), 1)).astype(F32)
    for way, table in enumerate((higher, lower)):
        spread = jnp.zeros((owners, total), F32)
        for mode in range(modes):
            link = table[mode : mode + 1, :]
            source = lax.div(link, count)
            local = (link - source * count).astype(F32)
            spread = spread + jnp.where(source == names, local, 0.0)
        found = dot(spread.astype(BF16), member.astype(BF16))
        picks[way * owners : (way + 1) * owners, :] = found.astype(jnp.int32)


def body(adjoint, saved, propagators, coupling, higher, lower, ladder, rates, decay):
    nodes = lax.axis_size("node")
    cores = lax.axis_size("cores")
    owners = nodes * cores
    own = lax.axis_index(("node", "cores"))
    count = adjoint.shape[0]
    modes = higher.shape[1]
    steps, subs = propagators.shape[:2]
    dim = coupling.shape[0]
    depth = 1 << (cores.bit_length() // 2)
    width = cores // depth
    lanes = nodes * width
    rows = dim // owners
    halves = 2 if subs % 2 == 0 else 1
    batch = subs // halves
    higher, lower, ladder = higher.T, lower.T, jnp.swapaxes(ladder, 1, 2)
    smem = pl.BlockSpec(memory_space=pltpu.SMEM)
    vmem = pl.BlockSpec(memory_space=pltpu.VMEM)
    picks = pl.pallas_call(
        functools.partial(pick_kernel, owners, count, modes),
        out_shape=jax.ShapeDtypeStruct((2 * owners, owners), jnp.int32),
        in_specs=[vmem, vmem],
        out_specs=vmem,
    )(higher, lower)
    block = adjoint.shape
    hbm = pl.BlockSpec(memory_space=pl.ANY)
    hops = depth - 1
    state, grad = pl.pallas_call(
        functools.partial(kernel, (nodes, depth, width, count, modes, steps, subs, dim, halves)),
        out_shape=(
            jax.ShapeDtypeStruct(block, BF16),
            jax.ShapeDtypeStruct((rows, steps * subs, 2, dim), F32),
        ),
        in_specs=[smem] * 6 + [vmem, hbm, vmem, vmem],
        out_specs=(hbm, vmem),
        scratch_shapes=[
            pltpu.VMEM((steps * subs, 2 * dim, 2 * dim), BF16),
            pltpu.VMEM((steps * subs, 2 * dim, 2 * dim), BF16),
            pltpu.VMEM((steps, subs + 1) + block, BF16),
            pltpu.VMEM((lanes - 1, depth, 2) + block[1:], BF16),
            pltpu.VMEM((owners, 2) + block[1:], BF16),
            pltpu.VMEM((batch, dim, 2 * dim), F32),
            pltpu.VMEM((steps * halves, owners, batch * rows, 2 * dim), BF16),
            pltpu.VMEM((steps * halves, owners - 1, batch * rows, 2 * dim), BF16),
            pltpu.VMEM(saved.shape, BF16),
            pltpu.VMEM((subs, dim, count * 2 * dim), BF16),
            *[pltpu.VMEM(block, BF16) for _ in range(2 * steps * hops)],
            pltpu.SemaphoreType.DMA((steps, 2, hops)),
            pltpu.SemaphoreType.DMA((steps, 2, hops)),
            pltpu.SemaphoreType.DMA((lanes - 1, depth)),
            pltpu.SemaphoreType.DMA((owners,)),
            pltpu.SemaphoreType.DMA((steps * halves,)),
            pltpu.SemaphoreType.DMA((steps * halves,)),
            pltpu.SemaphoreType.DMA((2,)),
            pltpu.SemaphoreType.REGULAR,
        ],
        compiler_params=pltpu.CompilerParams(
            collective_id=0, has_side_effects=True, vmem_limit_bytes=63_000_000
        ),
    )(picks, higher, lower, ladder, rates, decay, adjoint, saved, propagators, coupling)
    return state, grad


def solution(mesh):
    return jax.shard_map(
        body,
        mesh=mesh,
        in_specs=(
            P(("node", "cores"), None, None, None),
            P(None, None, ("node", "cores"), None, None, None),
            P(),
            P(),
            P(),
            P(),
            P(None, ("node", "cores"), None),
            P(),
            P(("node", "cores")),
        ),
        out_specs=(P(("node", "cores"), None, None, None), P(("node", "cores"), None, None, None)),
        check_vma=False,
    )
```

```python
import functools

import jax
import jax.numpy as jnp
from jax import lax
from jax.experimental import pallas as pl
from jax.experimental.pallas import tpu as pltpu
from jax.sharding import PartitionSpec as P

MESH = pl.DeviceIdType.MESH
F32 = jnp.float32
BF16 = jnp.bfloat16


def dot(a, b):
    return jnp.dot(a, b, preferred_element_type=F32)


def kernel(
    dims,
    picks,
    higher,
    lower,
    ladder,
    rates,
    decay,
    adjoint,
    saved_in,
    propagators,
    coupling,
    out,
    grad,
    right_u,
    left_u,
    hist,
    stage,
    inbox,
    terms,
    term_stage,
    term_inbox,
    saved,
    saved_t,
    *rest,
):
    nodes, depth, width, count, modes, steps, subs, dim, halves = dims
    hops = depth - 1
    chain = rest[: 2 * steps * hops]
    chain_send, chain_recv, plane_send, plane_recv, term_send, term_recv, local, credit = rest[
        2 * steps * hops :
    ]
    cores = depth * width
    owners = nodes * cores
    lanes = nodes * width
    rows = dim // owners
    batch = subs // halves
    node = lax.axis_index("node")
    spot = lax.axis_index("cores")
    level = spot // width
    column = spot % width
    lane = node * width + column

    def lane_of(offset):
        pair = 2 if nodes % 2 == 0 else 1
        far = lax.rem(node // pair + offset // (pair * width), nodes // pair)
        near = lax.rem(node + offset // width, pair)
        return (far * pair + near) * width + lax.rem(column + offset, width)

    def lane_id(other):
        return (other // width, level * width + other % width)

    def level_id(other):
        return (node, other * width + column)

    def owner_of(a_lane, a_level):
        return (a_lane // width) * cores + a_level * width + a_lane % width

    barrier = pltpu.get_barrier_semaphore()

    own = node * cores + spot

    def owner_id(offset):
        other = lax.rem(own + offset, owners)
        return (other // cores, lax.rem(other, cores))

    def greet(offset, carry):
        pl.semaphore_signal(barrier, inc=1, device_id=owner_id(offset), device_id_type=MESH)
        return carry

    lax.fori_loop(1, owners, greet, 0)
    fetch = pltpu.make_async_copy(saved_in, saved, local.at[0])
    fetch.start()

    def chain_block(step, way, hop):
        return chain[(step * 2 + way) * hops + hop - 1]

    def chain_copy(step, way, hop, source):
        peer = level + 1 if way == 0 else level - 1
        return pltpu.make_async_remote_copy(
            src_ref=source,
            dst_ref=chain_block(step, way, hop),
            send_sem=chain_send.at[step, way, hop - 1],
            recv_sem=chain_recv.at[step, way, hop - 1],
            device_id=level_id(peer),
            device_id_type=MESH,
        )

    def from_level(way, hop):
        return level - hop if way == 0 else level + hop

    def arrives(way, hop):
        return level >= hop if way == 0 else level + hop < depth

    def goes_on(way, hop):
        if way == 0:
            return jnp.logical_and(level >= hop - 1, level < depth - 1)
        return jnp.logical_and(level + hop - 1 < depth, level > 0)

    def plane_copy(offset, a_level):
        return pltpu.make_async_remote_copy(
            src_ref=stage.at[offset - 1, a_level],
            dst_ref=inbox.at[owner_of(lane, a_level)],
            send_sem=plane_send.at[offset - 1, a_level],
            recv_sem=plane_recv.at[owner_of(lane, a_level)],
            device_id=lane_id(lane_of(offset)),
            device_id_type=MESH,
        )

    def serve(block, a_level):
        fill_stage(block, a_level)
        send_stage(a_level)

    def fill_stage(block, a_level):
        source = owner_of(lane, a_level)

        def pick(offset, way):
            target = owner_of(lane_of(offset), level)
            return picks[way * owners + source, target]

        for way in range(2):
            inbox[source, way] = block[pick(0, way)]

        def fill(offset, carry):
            for way in range(2):
                stage[offset - 1, a_level, way] = block[pick(offset, way)]
            return carry

        lax.fori_loop(1, lanes, fill, 0)

    def send_stage(a_level):
        def send(offset, carry):
            plane_copy(offset, a_level).start()
            return carry

        lax.fori_loop(1, lanes, send, 0)

    def prepare():
        def one(at, carry):
            step, sub = at // subs, at % subs
            u_re = propagators[step, sub, 0]
            u_im = propagators[step, sub, 1]
            right_u[at, :dim, :dim] = u_re
            right_u[at, :dim, dim:] = u_im
            right_u[at, dim:, :dim] = -u_im
            right_u[at, dim:, dim:] = u_re
            t_re = u_re.T
            t_im = u_im.T
            left_u[at, :dim, :dim] = t_re
            left_u[at, :dim, dim:] = t_im
            left_u[at, dim:, :dim] = -t_im
            left_u[at, dim:, dim:] = t_re
            return carry

        lax.fori_loop(0, steps * subs, one, 0)

    def turn(sub):
        for j in range(count):
            kept = saved[steps - 1, sub, j].reshape(2 * dim, dim)
            saved_t[sub, :, 2 * dim * j : 2 * dim * (j + 1)] = kept.T

    def project(step, sub):
        total = jnp.zeros((dim, 2 * dim), F32)
        for j in range(count):
            lam_re = hist[step, sub + 1, j, 0]
            lam_im = hist[step, sub + 1, j, 1]
            both = jnp.concatenate(
                [
                    jnp.concatenate([lam_re, lam_im], axis=1),
                    jnp.concatenate([lam_im, -lam_re], axis=1),
                ],
                axis=0,
            )
            if step == steps - 1:
                kept_t = saved_t[sub, :, 2 * dim * j : 2 * dim * (j + 1)]
                total = total + dot(kept_t, both)
            else:
                kept = saved[step, sub, j].reshape(2 * dim, dim)
                total = total + lax.dot_general(
                    kept, both, (((0,), (0,)), ((), ())), preferred_element_type=F32
                )
        terms[sub % batch] = total
        if sub % batch == batch - 1:
            spread(step * halves + sub // batch)

    def spread(group):
        for target in range(owners):
            term_stage[group, target] = jnp.concatenate(
                [terms[i, target * rows : (target + 1) * rows] for i in range(batch)], axis=0
            ).astype(BF16)

        def send(offset, carry):
            pltpu.make_async_remote_copy(
                src_ref=term_stage.at[group, lax.rem(own + offset, owners)],
                dst_ref=term_inbox.at[group, offset - 1],
                send_sem=term_send.at[group],
                recv_sem=term_recv.at[group],
                device_id=owner_id(offset),
                device_id_type=MESH,
            ).start()
            return carry

        lax.fori_loop(1, owners, send, 0)

    def finish(group):
        everything = term_inbox.at[group]
        pltpu.make_async_copy(everything, everything, term_recv.at[group]).wait()
        total = term_stage[group, own].astype(F32)
        for offset in range(1, owners):
            total = total + term_inbox[group, offset - 1].astype(F32)
        for i in range(batch):
            for row in range(rows):
                for part in range(2):
                    grad[row, group * batch + i, part : part + 1, :] = total[
                        i * rows + row : i * rows + row + 1, part * dim : (part + 1) * dim
                    ]
        pltpu.make_async_copy(everything, everything, term_send.at[group]).wait()

    def couple(step, state):
        operator = coupling[...]

        def one(j, carry):
            plus, minus = [], []
            for part in range(2):
                sums = []
                for way in range(2):
                    total = jnp.zeros((dim, dim), F32)
                    for mode in range(modes):
                        weight = ladder[way, mode, j].astype(F32) * rates[way, mode]
                        place = lax.div((higher, lower)[way][mode, own * count + j], count)
                        total = total + weight * inbox[place, way, part].astype(F32)
                    sums.append(total)
                plus.append((sums[0] + sums[1]).astype(BF16))
                minus.append((sums[0] - sums[1]).astype(BF16))
            left = dot(operator, jnp.concatenate([plus[1], -plus[0]], axis=1))
            right = dot(jnp.concatenate([minus[1], -minus[0]], axis=0), operator)
            for part in range(2):
                lam = decay[j] * state[j, part].astype(F32)
                lam = lam + left[:, part * dim : (part + 1) * dim]
                lam = lam - right[part * dim : (part + 1) * dim]
                hist[step, 0, j, part] = lam.astype(BF16)
            return carry

        lax.fori_loop(0, count, one, 0)

    def rotate(step, half):
        def one(sub, carry):
            at = step * subs + sub
            mult_r = right_u[at]
            mult_l = left_u[at]
            for j in range(0, count, 2):
                rows = jnp.concatenate(
                    [
                        jnp.concatenate(
                            [hist[step, sub, j + i, 0], hist[step, sub, j + i, 1]], axis=1
                        )
                        for i in range(2)
                    ],
                    axis=0,
                )
                middle = dot(rows, mult_r).astype(BF16)
                stacked = jnp.concatenate(
                    [
                        jnp.concatenate([middle[:dim, :dim], middle[dim:, :dim]], axis=1),
                        jnp.concatenate([middle[:dim, dim:], middle[dim:, dim:]], axis=1),
                    ],
                    axis=0,
                )
                result = dot(mult_l, stacked).astype(BF16)
                for i in range(2):
                    for part in range(2):
                        hist[step, sub + 1, j + i, part] = result[
                            part * dim : (part + 1) * dim, i * dim : (i + 1) * dim
                        ]
            return carry

        lax.fori_loop(half * batch, (half + 1) * batch, one, 0)

    prepare()
    fill_stage(adjoint, level)
    pl.semaphore_wait(barrier, owners - 1)
    for step in range(steps):
        state = adjoint if step == 0 else hist.at[step - 1, subs]
        for way in range(2):

            @pl.when(goes_on(way, 1))
            def _(way=way):
                chain_copy(step, way, 1, state).start()

        if step > 0:
            pl.semaphore_wait(credit, lanes - 1)
            fill_stage(state, level)
        send_stage(level)
        if step == 0:
            fetch.wait()
        beside = [[] for _ in range(depth)]
        for sub in range(subs):
            beside[sub * depth // subs].append(sub)

        def aside(place):
            for sub in beside[place]:
                if step > 0:
                    project(step - 1, sub)
                if step == 0:
                    turn(sub)

        aside(0)
        for hop in range(1, depth):
            for way in range(2):

                @pl.when(arrives(way, hop))
                def _(way=way, hop=hop):
                    block = chain_block(step, way, hop)
                    chain_copy(step, way, hop, block).wait_recv()
                    if hop + 1 < depth:

                        @pl.when(goes_on(way, hop + 1))
                        def _():
                            chain_copy(step, way, hop + 1, block).start()

                    serve(block, from_level(way, hop))

            aside(hop)

        def collect(offset, carry):
            for a_level in range(depth):
                source = owner_of(lane_of(offset), a_level)
                pltpu.make_async_remote_copy(
                    src_ref=stage.at[offset - 1, a_level],
                    dst_ref=inbox.at[source],
                    send_sem=plane_send.at[offset - 1, a_level],
                    recv_sem=plane_recv.at[source],
                    device_id=lane_id(lane_of(offset)),
                    device_id_type=MESH,
                ).wait_recv()
            return carry

        lax.fori_loop(1, lanes, collect, 0)
        couple(step, state)
        if step + 1 < steps:

            def allow(offset, carry):
                pl.semaphore_signal(
                    credit, inc=1, device_id=lane_id(lane_of(offset)), device_id_type=MESH
                )
                return carry

            lax.fori_loop(1, lanes, allow, 0)
        for half in range(halves):
            rotate(step, half)
            if step == steps - 1:
                for sub in range(half * batch, (half + 1) * batch):
                    project(step, sub)
                    if sub == subs - 1:
                        result = pltpu.make_async_copy(hist.at[step, subs], out, local.at[1])
                        result.start()

        def settle(offset, carry):
            for a_level in range(depth):
                plane_copy(offset, a_level).wait_send()
            return carry

        lax.fori_loop(1, lanes, settle, 0)
        for hop in range(1, depth):
            for way in range(2):

                @pl.when(goes_on(way, hop))
                def _(way=way, hop=hop):
                    chain_copy(step, way, hop, chain_block(step, way, hop)).wait_send()

    result.wait()
    for group in range(steps * halves):
        finish(group)


def pick_kernel(owners, count, modes, higher, lower, picks):
    total = owners * count
    names = lax.broadcasted_iota(jnp.int32, (owners, total), 0)
    member = lax.div(lax.broadcasted_iota(jnp.int32, (total, owners), 0), count)
    member = (member == lax.broadcasted_iota(jnp.int32, (total, owners), 1)).astype(F32)
    for way, table in enumerate((higher, lower)):
        spread = jnp.zeros((owners, total), F32)
        for mode in range(modes):
            link = table[mode : mode + 1, :]
            source = lax.div(link, count)
            local = (link - source * count).astype(F32)
            spread = spread + jnp.where(source == names, local, 0.0)
        found = dot(spread.astype(BF16), member.astype(BF16))
        picks[way * owners : (way + 1) * owners, :] = found.astype(jnp.int32)


def body(adjoint, saved, propagators, coupling, higher, lower, ladder, rates, decay):
    nodes = lax.axis_size("node")
    cores = lax.axis_size("cores")
    owners = nodes * cores
    own = lax.axis_index(("node", "cores"))
    count = adjoint.shape[0]
    modes = higher.shape[1]
    steps, subs = propagators.shape[:2]
    dim = coupling.shape[0]
    depth = 1 << (cores.bit_length() // 2)
    width = cores // depth
    lanes = nodes * width
    rows = dim // owners
    halves = 2 if subs % 2 == 0 else 1
    batch = subs // halves
    higher, lower, ladder = higher.T, lower.T, jnp.swapaxes(ladder, 1, 2)
    smem = pl.BlockSpec(memory_space=pltpu.SMEM)
    vmem = pl.BlockSpec(memory_space=pltpu.VMEM)
    picks = pl.pallas_call(
        functools.partial(pick_kernel, owners, count, modes),
        out_shape=jax.ShapeDtypeStruct((2 * owners, owners), jnp.int32),
        in_specs=[vmem, vmem],
        out_specs=vmem,
    )(higher, lower)
    block = adjoint.shape
    hbm = pl.BlockSpec(memory_space=pl.ANY)
    hops = depth - 1
    state, grad = pl.pallas_call(
        functools.partial(kernel, (nodes, depth, width, count, modes, steps, subs, dim, halves)),
        out_shape=(
            jax.ShapeDtypeStruct(block, BF16),
            jax.ShapeDtypeStruct((rows, steps * subs, 2, dim), F32),
        ),
        in_specs=[smem] * 6 + [vmem, hbm, vmem, vmem],
        out_specs=(hbm, vmem),
        scratch_shapes=[
            pltpu.VMEM((steps * subs, 2 * dim, 2 * dim), BF16),
            pltpu.VMEM((steps * subs, 2 * dim, 2 * dim), BF16),
            pltpu.VMEM((steps, subs + 1) + block, BF16),
            pltpu.VMEM((lanes - 1, depth, 2) + block[1:], BF16),
            pltpu.VMEM((owners, 2) + block[1:], BF16),
            pltpu.VMEM((batch, dim, 2 * dim), F32),
            pltpu.VMEM((steps * halves, owners, batch * rows, 2 * dim), BF16),
            pltpu.VMEM((steps * halves, owners - 1, batch * rows, 2 * dim), BF16),
            pltpu.VMEM(saved.shape, BF16),
            pltpu.VMEM((subs, dim, count * 2 * dim), BF16),
            *[pltpu.VMEM(block, BF16) for _ in range(2 * steps * hops)],
            pltpu.SemaphoreType.DMA((steps, 2, hops)),
            pltpu.SemaphoreType.DMA((steps, 2, hops)),
            pltpu.SemaphoreType.DMA((lanes - 1, depth)),
            pltpu.SemaphoreType.DMA((owners,)),
            pltpu.SemaphoreType.DMA((steps * halves,)),
            pltpu.SemaphoreType.DMA((steps * halves,)),
            pltpu.SemaphoreType.DMA((2,)),
            pltpu.SemaphoreType.REGULAR,
        ],
        compiler_params=pltpu.CompilerParams(
            collective_id=0, has_side_effects=True, vmem_limit_bytes=63_000_000
        ),
    )(picks, higher, lower, ladder, rates, decay, adjoint, saved, propagators, coupling)
    return state, grad


def solution(mesh):
    return jax.shard_map(
        body,
        mesh=mesh,
        in_specs=(
            P(("node", "cores"), None, None, None),
            P(None, None, ("node", "cores"), None, None, None),
            P(),
            P(),
            P(),
            P(),
            P(None, ("node", "cores"), None),
            P(),
            P(("node", "cores")),
        ),
        out_specs=(P(("node", "cores"), None, None, None), P(("node", "cores"), None, None, None)),
        check_vma=False,
    )
```
